32 devices in a mesh: segment: 8 (over y, x, core), rows: 4 (over z).
Axes of the slice: x: 2, y: 2, z: 4, core: 2. Of those that a mesh axis runs over, the one named last changes fastest.
Arguments:
- held_maps: bfloat16 [8, 64, 64, 256], P('segment', 'rows'), may hold values from -6 to 6
- held_skips: bfloat16 [3, 8, 64, 64, 256], P(None, 'segment', 'rows'), may hold values from -6 to 6
- arrivals: bfloat16 [3, 64, 64, 256], P(None, 'rows'), may hold values from -6 to 6
- kernels: bfloat16 [8, 3, 3, 768, 256], P('segment'), may hold values from -0.125 to 0.125
- biases: float32 [8, 3, 256], P('segment'), may hold values from -3 to 3
Outputs:
- section_maps: bfloat16 [3, 8, 64, 64, 256], P(None, 'segment', 'rows')
- skip_stash: bfloat16 [3, 8, 64, 64, 256], P(None, 'segment', 'rows')
The draws below stay inside these ranges and needn't reach their ends.
All inputs are finite; a program needn't handle non-finite values.
Results may differ from the reference program's by a relative error of at most 0.0075.
Values may be sent and summed in bfloat16 or wider, within the bound.
A program may use at most 64 MiB of HBM per device.

```python
import jax
import jax.numpy as jnp
from jax import lax

C = 256
W = 64
TICKS = 3
CONVS = 3
H = 64
N_SEGMENT = 8


def shard_levels(stream_key, dims, shards, least, top_value):
    level, own = 1.0, jax.random.fold_in(stream_key, 6)
    for dim, parts in shards:
        draws = jnp.exp(jax.random.uniform(jax.random.fold_in(own, dim), (parts,), jnp.float32, least / len(shards), top_value / len(shards)))
        level = level * jnp.repeat(draws, dims[dim] // parts).reshape([-1 if axis == dim else 1 for axis in range(len(dims))])
    return level


def gaussian(own_key, shape, width, bound, shards=(), held_as=jnp.bfloat16):
    values = width * jax.random.normal(own_key, shape, jnp.float32)
    if shards:
        values = values * shard_levels(own_key, shape, shards, -0.22, 0.18)
    return jnp.clip(values, -bound, bound).astype(held_as)


def setup_inputs(seed: int = 0) -> dict:
    arg_keys = jax.random.split(jax.random.key(seed), 6)
    held_maps = gaussian(arg_keys[0], (N_SEGMENT, H, W, C), 1.0, 6.0, ((0, 8), (1, 4)))
    held_skips = gaussian(arg_keys[1], (TICKS, N_SEGMENT, H, W, C), 1.0, 6.0, ((1, 8), (2, 4)))
    arrivals = gaussian(arg_keys[2], (TICKS, H, W, C), 1.0, 6.0, ((1, 4),))
    kernels = gaussian(arg_keys[3], (N_SEGMENT, CONVS, 3, 3 * C, C), (9 * C) ** -0.5, 0.125, ((0, 8),))
    biases = gaussian(arg_keys[4], (N_SEGMENT, CONVS, C), 0.5, 3.0, ((0, 8),), jnp.float32)
    return {"held_maps": held_maps, "held_skips": held_skips, "arrivals": arrivals, "kernels": kernels, "biases": biases}


def convolve(source, kernel, offsets):
    rows_out = source.shape[0] - 2
    columns_count = source.shape[1]
    padded = jnp.pad(source, ((0, 0), (1, 1), (0, 0)))
    columns = jnp.concatenate([padded[:, 0:columns_count], padded[:, 1:columns_count + 1], padded[:, 2:columns_count + 2]], axis=-1)
    summed = jnp.zeros((rows_out * columns_count, kernel.shape[2]), jnp.float32)
    for row_offset in range(3):
        block = columns[row_offset:row_offset + rows_out].reshape(rows_out * columns_count, -1)
        summed = summed + jnp.dot(block, kernel[row_offset], preferred_element_type=jnp.float32)
    return summed.reshape(rows_out, columns_count, -1) + offsets


def pad_rows(source):
    return jnp.pad(source, ((1, 1), (0, 0), (0, 0)))


def run_section(operands):
    section_in, kernel, offsets = operands
    hidden_state = section_in
    for layer_index in range(2):
        hidden_state = jax.nn.silu(convolve(pad_rows(hidden_state), kernel[layer_index], offsets[layer_index])).astype(jnp.bfloat16)
    summed = section_in.astype(jnp.float32) + convolve(pad_rows(hidden_state), kernel[2], offsets[2])
    return summed.astype(jnp.bfloat16)


def reference(held_maps, held_skips, arrivals, kernels, biases):
    previous = held_maps
    half = N_SEGMENT // 2
    section_results = []
    stored_skips = []
    for tick in range(TICKS):
        incoming = jnp.concatenate([arrivals[tick][None], previous[:-1]], axis=0)
        joined = []
        for section in range(N_SEGMENT):
            if section < half:
                joined.append(incoming[section])
            else:
                delay = 2 * section - N_SEGMENT + 1
                if tick >= delay:
                    skip = section_results[tick - delay][N_SEGMENT - 1 - section]
                else:
                    skip = held_skips[tick, section]
                joined.append((incoming[section].astype(jnp.float32) + skip.astype(jnp.float32)).astype(jnp.bfloat16))
        section_in = jnp.stack(joined)
        new_activation = lax.map(run_section, (section_in, kernels, biases))
        section_results.append(new_activation)
        decoder_marker = (jnp.arange(N_SEGMENT) >= half)[:, None, None, None]
        stored_skips.append(jnp.where(decoder_marker, new_activation[::-1], jnp.zeros_like(new_activation)))
        previous = new_activation
    return jnp.stack(section_results), jnp.stack(stored_skips)
```

```python
import functools

import jax
import jax.numpy as jnp
from jax import lax
from jax.experimental import pallas as pl
from jax.experimental.pallas import tpu as pltpu
from jax.sharding import PartitionSpec as P

BF16 = jnp.bfloat16
F32 = jnp.float32


def split(total, most):
    parts = -(-total // most)
    sizes = [total // parts + (1 if i < total % parts else 0) for i in range(parts)]
    out, at = [], 0
    for size in sizes:
        out.append((at, size))
        at += size
    return out


def body(
    ticks, rows, w, c,
    held, skips_in, arrivals, kern, bias,
    maps, stash,
    inc, sk, sec, halo, kv, x0, x1, x2, outb,
    inc_rs, shift_ss, halo_ss, halo_rs, st_ss, st_rs, fwd_ss, out_s, k_s, sk_s,
):
    n = lax.axis_size("segment")
    nz = lax.axis_size("rows")
    s = lax.axis_index("segment")
    z = lax.axis_index("rows")
    half = n // 2
    last = ticks - 1
    encoder = s < half
    decoder = s >= half
    middle = s == half
    has_next = s < n - 1
    has_prev = s >= 1
    has_up = z >= 1
    has_down = z < nz - 1
    relayed = encoder & (s % 2 == 1) & (s < half - 1)
    relays = encoder & (s % 2 == 0) & (s >= 2)
    from_relay = (s > half) & (s % 2 == 0)
    direct = encoder & (s % 2 == 0) & (s < half - 1)
    mirror = n - 1 - s
    q = rows // 4
    pieces = ((0, q), (rows - q, q), (q, rows - 2 * q))

    def at(segment, row):
        return {"segment": segment, "rows": row}

    barrier = pltpu.get_barrier_semaphore()
    links = (
        (has_next, s + 1, z),
        (has_prev, s - 1, z),
        (encoder | decoder, mirror, z),
        (relays | from_relay, n - s, z),
        (has_up, s, z - 1),
        (has_down, s, z + 1),
    )
    partners = 0
    for cond, seg, row in links:
        @pl.when(cond)
        def _():
            pl.semaphore_signal(barrier, inc=1, device_id=at(seg, row), device_id_type=pl.DeviceIdType.MESH)
        partners = partners + cond.astype(jnp.int32)

    k_copies = [pltpu.make_async_copy(kern.at[l], kv.at[l], k_s.at[l]) for l in range(3)]
    for copy in k_copies:
        copy.start()
    skip_copy = pltpu.make_async_copy(skips_in, sk, sk_s.at[0])

    @pl.when(decoder)
    def _():
        skip_copy.start()

    @pl.when(s == 0)
    def _():
        for t in range(ticks):
            for p, (r, m) in enumerate(pieces):
                pltpu.make_async_copy(
                    arrivals.at[t, pl.ds(r * w, m * w)], inc.at[t, pl.ds(r * w, m * w)], inc_rs.at[t, p]
                ).start()

    pl.semaphore_wait(barrier, partners)

    def remote(src, dst, ss, rs, seg, row):
        return pltpu.make_async_remote_copy(
            src_ref=src, dst_ref=dst, send_sem=ss, recv_sem=rs, device_id=at(seg, row),
            device_id_type=pl.DeviceIdType.MESH,
        )

    def shift_copy(src, t, p):
        r, m = pieces[p]
        rng = pl.ds(r * w, m * w)
        return remote(src.at[rng], inc.at[t, rng], shift_ss.at[t, p], inc_rs.at[t, p], s + 1, z)

    def stash_copy(t, p):
        r, m = pieces[p]
        rng = pl.ds(r * w, m * w)
        return remote(outb.at[t, rng], stash.at[t, rng], st_ss.at[t, p], st_rs.at[t, p], mirror, z)

    def relay_copy(t, p):
        r, m = pieces[p]
        rng = pl.ds(r * w, m * w)
        return remote(inc.at[t + 1, rng], stash.at[t, rng], fwd_ss.at[t, p], st_rs.at[t, p], n - s, z)

    def keep_copy(t, p):
        r, m = pieces[p]
        rng = pl.ds(r * w, m * w)
        return pltpu.make_async_copy(inc.at[t + 1, rng], stash.at[t, rng], st_rs.at[t, p])

    @pl.when(has_next)
    def _():
        for p in range(3):
            shift_copy(held, 0, p).start()

    e = 3 * w

    def up_copy(t):
        return remote(sec.at[t, 0], halo.at[t, 1], halo_ss.at[t, 0], halo_rs.at[t, 1], s, z - 1)

    def down_copy(t):
        return remote(sec.at[t, 1], halo.at[t, 0], halo_ss.at[t, 1], halo_rs.at[t, 0], s, z + 1)

    @pl.when(encoder)
    def _():
        sk[...] = jnp.zeros_like(sk)

    @pl.when(jnp.logical_not(has_up))
    def _():
        for t in range(ticks):
            halo[t, 0] = jnp.zeros((e, c), BF16)

    @pl.when(jnp.logical_not(has_down))
    def _():
        for t in range(ticks):
            halo[t, 1] = jnp.zeros((e, c), BF16)

    def put(dst, row, a):
        m = a.shape[0]
        col = lax.rem(lax.broadcasted_iota(jnp.int32, a.shape, 0), w)
        rng = pl.ds(row * w, m)
        dst[rng, c : 2 * c] = a.astype(BF16)
        dst[rng, 0:c] = jnp.where(col == 0, 0.0, pltpu.roll(a, 1, 0)).astype(BF16)
        dst[rng, 2 * c : 3 * c] = jnp.where(col == w - 1, 0.0, pltpu.roll(a, m - 1, 0)).astype(BF16)

    def patches(src, base, count):
        return jnp.concatenate([src[pl.ds((base + d) * w, count * w), :] for d in range(3)], axis=1)

    def conv(lhs, l):
        return jnp.dot(lhs, kv[l], preferred_element_type=F32) + bias[pl.ds(l, 1), :]

    def silu(v):
        return v / (1.0 + jnp.exp(-v))

    up_i = has_up.astype(jnp.int32)
    down_i = has_down.astype(jnp.int32)

    for t in range(ticks):
        mid_t = middle if t >= 1 else None

        def joined(r, m):
            rng = pl.ds(r * w, m * w)
            x = inc[t, rng].astype(F32)
            add = sk[t, rng].astype(F32)
            if mid_t is not None:
                add = jnp.where(mid_t, x, add)
            return (x + add).astype(BF16)

        def arrived(p):
            r, m = pieces[p]
            view = inc.at[t, pl.ds(r * w, m * w)]
            pltpu.make_async_copy(view, view, inc_rs.at[t, p]).wait()
            if t >= 1:
                @pl.when(relays)
                def _():
                    relay_copy(t - 1, p).start()

                @pl.when(middle)
                def _():
                    keep_copy(t - 1, p).start()

        if t == 0:
            @pl.when(decoder)
            def _():
                skip_copy.wait()

        arrived(0)
        top = joined(0, q)
        sec[t, 0] = top[0:e]

        @pl.when(has_up)
        def _():
            up_copy(t).start()

        put(x0, 3, top.astype(F32))
        arrived(1)
        bottom = joined(rows - q, q)
        sec[t, 1] = bottom[q * w - e :]

        @pl.when(has_down)
        def _():
            down_copy(t).start()

        put(x0, 3 + rows - q, bottom.astype(F32))
        arrived(2)
        for r, m in split(rows - 2 * q, 4):
            put(x0, 3 + q + r, joined(q + r, m).astype(F32))
        if t == 0:
            k_copies[0].wait()
        for r, m in split(rows - 2, 7):
            put(x1, 3 + r, silu(conv(patches(x0, 3 + r, m), 0)))

        @pl.when(has_down)
        def _():
            remote(sec.at[t, 0], halo.at[t, 1], halo_ss.at[t, 0], halo_rs.at[t, 1], s, z).wait_recv()

        @pl.when(has_up)
        def _():
            remote(sec.at[t, 1], halo.at[t, 0], halo_ss.at[t, 1], halo_rs.at[t, 0], s, z).wait_recv()

        put(x0, 0, halo[t, 0].astype(F32))
        put(x0, 3 + rows, halo[t, 1].astype(F32))
        edge = silu(conv(jnp.concatenate([patches(x0, 0, 3), patches(x0, rows + 1, 3)], axis=0), 0))
        idx = lax.broadcasted_iota(jnp.int32, edge.shape, 0)
        inside = jnp.where(idx < 2 * w, up_i, jnp.where(idx >= 4 * w, down_i, 1)) > 0
        edge = jnp.where(inside, edge, 0.0)
        put(x1, 0, edge[0:e])
        put(x1, rows + 1, edge[e:])

        if t == 0:
            k_copies[1].wait()
        for r, m in split(rows + 2, 6):
            a = silu(conv(patches(x1, r, m), 1))
            if r == 0 or r + m == rows + 2:
                idx = lax.broadcasted_iota(jnp.int32, a.shape, 0)
                inside = jnp.where(idx < w, up_i, 1) if r == 0 else jnp.where(idx >= (m - 1) * w, down_i, 1)
                a = jnp.where(inside > 0, a, 0.0)
            put(x2, r, a)

        if t == 0:
            k_copies[2].wait()

        def emit(p):
            if t < last:
                @pl.when(has_next)
                def _():
                    shift_copy(outb.at[t], t + 1, p).start()

                @pl.when(direct)
                def _():
                    stash_copy(t, p).start()
            else:
                @pl.when(encoder)
                def _():
                    stash_copy(t, p).start()

        def own(r, m):
            return x0[pl.ds((3 + r) * w, m * w), c : 2 * c].astype(F32)

        ends = conv(jnp.concatenate([patches(x2, 0, q), patches(x2, rows - q, q)], axis=0), 2)
        outb[t, 0 : q * w] = (own(0, q) + ends[0 : q * w]).astype(BF16)
        emit(0)
        outb[t, (rows - q) * w :] = (own(rows - q, q) + ends[q * w :]).astype(BF16)
        emit(1)
        for r, m in split(rows - 2 * q, 8):
            outb[t, pl.ds((q + r) * w, m * w)] = (own(q + r, m) + conv(patches(x2, q + r, m), 2)).astype(BF16)
        emit(2)
        pltpu.make_async_copy(outb.at[t], maps.at[t], out_s.at[t]).start()

    for t in range(ticks):
        @pl.when(has_up)
        def _():
            up_copy(t).wait_send()

        @pl.when(has_down)
        def _():
            down_copy(t).wait_send()

        for p in range(3):
            @pl.when(has_next)
            def _():
                shift_copy(held if t == 0 else outb.at[t - 1], t, p).wait_send()

            if t < last:
                @pl.when(relays)
                def _():
                    relay_copy(t, p).wait_send()

                @pl.when(direct)
                def _():
                    stash_copy(t, p).wait_send()

                @pl.when(decoder)
                def _():
                    keep_copy(t, p).wait()
            else:
                @pl.when(encoder)
                def _():
                    stash_copy(t, p).wait_send()

                @pl.when(decoder)
                def _():
                    stash_copy(t, p).wait_recv()
        pltpu.make_async_copy(outb.at[t], maps.at[t], out_s.at[t]).wait()


def on_device(held_maps, held_skips, arrivals, kernels, biases):
    ticks, _, rows, w, c = held_skips.shape
    flat = rows * w
    any_spec = pl.BlockSpec(memory_space=pl.ANY)
    shape = jax.ShapeDtypeStruct((ticks, flat, c), BF16)
    dma = pltpu.SemaphoreType.DMA
    maps, stash = pl.pallas_call(
        functools.partial(body, ticks, rows, w, c),
        out_shape=(shape, shape),
        in_specs=[any_spec] * 4 + [pl.BlockSpec(memory_space=pltpu.VMEM)],
        out_specs=(any_spec, any_spec),
        scratch_shapes=[
            pltpu.VMEM((ticks, flat, c), BF16),
            pltpu.VMEM((ticks, flat, c), BF16),
            pltpu.VMEM((ticks, 2, 3 * w, c), BF16),
            pltpu.VMEM((ticks, 2, 3 * w, c), BF16),
            pltpu.VMEM((3, 9 * c, c), BF16),
            pltpu.VMEM(((rows + 6) * w, 3 * c), BF16),
            pltpu.VMEM(((rows + 4) * w, 3 * c), BF16),
            pltpu.VMEM(((rows + 2) * w, 3 * c), BF16),
            pltpu.VMEM((ticks, flat, c), BF16),
            dma((ticks, 3)),
            dma((ticks, 3)),
            dma((ticks, 2)),
            dma((ticks, 2)),
            dma((ticks, 3)),
            dma((ticks, 3)),
            dma((ticks, 3)),
            dma((ticks,)),
            dma((3,)),
            dma((1,)),
        ],
        compiler_params=pltpu.CompilerParams(
            collective_id=0, has_side_effects=True, vmem_limit_bytes=48 * 1024 * 1024
        ),
    )(
        held_maps.reshape(flat, c),
        held_skips.reshape(ticks, flat, c),
        arrivals.reshape(ticks, flat, c),
        kernels.reshape(3, 9 * c, c),
        biases[0],
    )
    decoder = lax.axis_index("segment") >= lax.axis_size("segment") // 2
    stash = jnp.where(decoder, stash, jnp.zeros_like(stash))
    full = (ticks, 1, rows, w, c)
    return maps.reshape(full), stash.reshape(full)


def solution(mesh):
    placed = (
        P("segment", "rows", None, None),
        P(None, "segment", "rows", None, None),
        P(None, "rows", None, None),
        P("segment", None, None, None, None),
        P("segment", None, None),
    )
    return jax.shard_map(
        on_device,
        mesh=mesh,
        in_specs=placed,
        out_specs=(P(None, "segment", "rows", None, None), P(None, "segment", "rows", None, None)),
        check_vma=False,
    )
```

```python
import functools

import jax
import jax.numpy as jnp
from jax import lax
from jax.experimental import pallas as pl
from jax.experimental.pallas import tpu as pltpu
from jax.sharding import PartitionSpec as P

BF16 = jnp.bfloat16
F32 = jnp.float32


def body(
    ticks, rows, w, c,
    held, skips_in, arrivals, kern, bias_in,
    maps, stash,
    inc, sk, sec, halo, kv, bias, x0, x1, x2, outb,
    inc_rs, shift_ss, halo_ss, halo_rs, st_ss, st_rs, fwd_ss, out_s, k_s, sk_s, b_s,
):
    n = lax.axis_size("segment")
    nz = lax.axis_size("rows")
    s = lax.axis_index("segment")
    z = lax.axis_index("rows")
    half = n // 2
    last = ticks - 1
    encoder = s < half
    decoder = s >= half
    middle = s == half
    has_next = s < n - 1
    has_prev = s >= 1
    has_up = z >= 1
    has_down = z < nz - 1
    relayed = encoder & (s % 2 == 1) & (s < half - 1)
    relays = encoder & (s % 2 == 0) & (s >= 2)
    from_relay = (s > half) & (s % 2 == 0)
    direct = encoder & (s % 2 == 0) & (s < half - 1)
    mirror = n - 1 - s
    q = 3
    h = (rows - 2 * q + 1) // 2
    pieces = ((0, q), (rows - q, q), (q, h), (q + h, rows - 2 * q - h))
    count = len(pieces)

    def at(segment, row):
        return {"segment": segment, "rows": row}

    barrier = pltpu.get_barrier_semaphore()
    links = (
        (has_next, s + 1, z),
        (has_prev, s - 1, z),
        (encoder | decoder, mirror, z),
        (relays | from_relay, n - s, z),
        (has_up, s, z - 1),
        (has_down, s, z + 1),
    )
    partners = 0
    for cond, seg, row in links:
        @pl.when(cond)
        def _():
            pl.semaphore_signal(barrier, inc=1, device_id=at(seg, row), device_id_type=pl.DeviceIdType.MESH)
        partners = partners + cond.astype(jnp.int32)

    k_copies = [pltpu.make_async_copy(kern.at[l], kv.at[l], k_s.at[l]) for l in range(3)]
    for copy in k_copies:
        copy.start()
    bias_copy = pltpu.make_async_copy(bias_in, bias, b_s.at[0])
    bias_copy.start()
    skip_copy = pltpu.make_async_copy(skips_in, sk, sk_s.at[0])

    @pl.when(decoder)
    def _():
        skip_copy.start()

    @pl.when(s == 0)
    def _():
        for t in range(ticks):
            for p, (r, m) in enumerate(pieces):
                pltpu.make_async_copy(
                    arrivals.at[t, pl.ds(r * w, m * w)], inc.at[t, pl.ds(r * w, m * w)], inc_rs.at[t, p]
                ).start()

    pl.semaphore_wait(barrier, partners)

    def remote(src, dst, ss, rs, seg, row):
        return pltpu.make_async_remote_copy(
            src_ref=src, dst_ref=dst, send_sem=ss, recv_sem=rs, device_id=at(seg, row),
            device_id_type=pl.DeviceIdType.MESH,
        )

    def shift_copy(src, t, p):
        r, m = pieces[p]
        rng = pl.ds(r * w, m * w)
        return remote(src.at[rng], inc.at[t, rng], shift_ss.at[t, p], inc_rs.at[t, p], s + 1, z)

    def stash_copy(t, p):
        r, m = pieces[p]
        rng = pl.ds(r * w, m * w)
        return remote(outb.at[t, rng], stash.at[t, rng], st_ss.at[t, p], st_rs.at[t, p], mirror, z)

    def relay_copy(t, p):
        r, m = pieces[p]
        rng = pl.ds(r * w, m * w)
        return remote(inc.at[t + 1, rng], stash.at[t, rng], fwd_ss.at[t, p], st_rs.at[t, p], n - s, z)

    def keep_copy(t, p):
        r, m = pieces[p]
        rng = pl.ds(r * w, m * w)
        return pltpu.make_async_copy(inc.at[t + 1, rng], stash.at[t, rng], st_rs.at[t, p])

    @pl.when(has_next)
    def _():
        for p in range(count):
            shift_copy(held, 0, p).start()

    e = 3 * w

    def up_copy(t):
        return remote(sec.at[t, 0], halo.at[t, 1], halo_ss.at[t, 0], halo_rs.at[t, 1], s, z - 1)

    def down_copy(t):
        return remote(sec.at[t, 1], halo.at[t, 0], halo_ss.at[t, 1], halo_rs.at[t, 0], s, z + 1)

    @pl.when(encoder)
    def _():
        sk[...] = jnp.zeros_like(sk)

    @pl.when(jnp.logical_not(has_up))
    def _():
        for t in range(ticks):
            halo[t, 0] = jnp.zeros((e, c), BF16)

    @pl.when(jnp.logical_not(has_down))
    def _():
        for t in range(ticks):
            halo[t, 1] = jnp.zeros((e, c), BF16)

    def put(dst, row, a):
        m = a.shape[0]
        rng = pl.ds(row * w, m)
        dst[rng, c : 2 * c] = a.astype(BF16)
        sub = lax.broadcasted_iota(jnp.int32, (m // w, 8, c), 1)
        left = pltpu.roll(a, 1, 0).reshape(m // w, w, c)
        first = jnp.where(sub == 0, 0.0, left[:, 0:8])
        dst[rng, 0:c] = jnp.concatenate([first, left[:, 8:]], axis=1).reshape(m, c).astype(BF16)
        right = pltpu.roll(a, m - 1, 0).reshape(m // w, w, c)
        final = jnp.where(sub == 7, 0.0, right[:, w - 8 :])
        dst[rng, 2 * c : 3 * c] = jnp.concatenate([right[:, 0 : w - 8], final], axis=1).reshape(m, c).astype(BF16)

    def patches(src, spans):
        return jnp.concatenate(
            [jnp.concatenate([src[pl.ds((b + d) * w, m * w), :] for b, m in spans], axis=0) for d in range(3)], axis=1
        )

    def silu(v):
        return v * (0.5 + 0.5 * jnp.tanh(0.5 * v))

    up_i = has_up.astype(jnp.int32)
    down_i = has_down.astype(jnp.int32)
    pending = []

    def flush():
        while pending:
            pending.pop(0)()

    def step(src, spans, l, finish):
        acc = jnp.dot(patches(src, spans), kv[l], preferred_element_type=F32)
        flush()
        pending.append(lambda: finish(acc + bias[l]))

    def store(dst, shift, spans, guard=0):
        def finish(v):
            v = silu(v)
            if guard:
                idx = lax.broadcasted_iota(jnp.int32, v.shape, 0)
                low = jnp.where(idx < guard * w, up_i, 1)
                inside = jnp.where(idx >= v.shape[0] - guard * w, down_i, low)
                v = jnp.where(inside > 0, v, 0.0)
            at_row = 0
            for b, m in spans:
                put(dst, b + shift, v[at_row * w : (at_row + m) * w])
                at_row += m

        return finish

    for t in range(ticks):
        mid_t = middle if t >= 1 else None

        def joined(p):
            r, m = pieces[p]
            rng = pl.ds(r * w, m * w)
            x = inc[t, rng].astype(F32)
            add = sk[t, rng].astype(F32)
            if mid_t is not None:
                add = jnp.where(mid_t, x, add)
            return (x + add).astype(BF16)

        def arrived(p):
            r, m = pieces[p]
            view = inc.at[t, pl.ds(r * w, m * w)]
            pltpu.make_async_copy(view, view, inc_rs.at[t, p]).wait()
            if t >= 1:
                @pl.when(relays)
                def _():
                    relay_copy(t - 1, p).start()

                @pl.when(middle)
                def _():
                    keep_copy(t - 1, p).start()

        def emit(p):
            if t < last:
                @pl.when(has_next)
                def _():
                    shift_copy(outb.at[t], t + 1, p).start()

                @pl.when(direct)
                def _():
                    stash_copy(t, p).start()
            else:
                @pl.when(encoder)
                def _():
                    stash_copy(t, p).start()

        def result(spans, ps):
            def finish(v):
                at_row = 0
                for b, m in spans:
                    own = x0[pl.ds((3 + b) * w, m * w), c : 2 * c].astype(F32)
                    outb[t, pl.ds(b * w, m * w)] = (own + v[at_row * w : (at_row + m) * w]).astype(BF16)
                    at_row += m
                for p in ps:
                    emit(p)

            return finish

        def spans_at(spans, base):
            return tuple((b + base, m) for b, m in spans)

        if t == 0:
            @pl.when(decoder)
            def _():
                skip_copy.wait()

        arrived(0)
        top = joined(0)
        sec[t, 0] = top

        @pl.when(has_up)
        def _():
            up_copy(t).start()

        arrived(1)
        bottom = joined(1)
        sec[t, 1] = bottom

        @pl.when(has_down)
        def _():
            down_copy(t).start()

        put(x0, 3, top.astype(F32))
        put(x0, 3 + rows - q, bottom.astype(F32))
        arrived(2)
        put(x0, 3 + pieces[2][0], joined(2).astype(F32))
        if t == 0:
            bias_copy.wait()
            k_copies[0].wait()
        a_end = q + h - 2
        first = ((1, a_end),)
        second = ((1 + a_end, rows - 2 - a_end),)
        step(x0, spans_at(first, 2), 0, store(x1, 2, first))
        arrived(3)
        put(x0, 3 + pieces[3][0], joined(3).astype(F32))
        step(x0, spans_at(second, 2), 0, store(x1, 2, second))

        @pl.when(has_down)
        def _():
            remote(sec.at[t, 0], halo.at[t, 1], halo_ss.at[t, 0], halo_rs.at[t, 1], s, z).wait_recv()

        @pl.when(has_up)
        def _():
            remote(sec.at[t, 1], halo.at[t, 0], halo_ss.at[t, 1], halo_rs.at[t, 0], s, z).wait_recv()

        put(x0, 0, halo[t, 0].astype(F32))
        put(x0, 3 + rows, halo[t, 1].astype(F32))
        edge1 = ((-2, 3), (rows - 1, 3))
        step(x0, spans_at(edge1, 2), 0, store(x1, 2, edge1, 2))
        if t == 0:
            k_copies[1].wait()
        ring2 = ((2, 3), (rows - 5, 3))
        step(x1, spans_at(ring2, 1), 1, store(x2, 1, ring2))
        edge2 = ((-1, 3), (rows - 2, 3))
        step(x1, spans_at(edge2, 1), 1, store(x2, 1, edge2, 1))
        core2 = ((5, rows - 10),)
        step(x1, spans_at(core2, 1), 1, store(x2, 1, core2))
        if t == 0:
            k_copies[2].wait()
        ends = (pieces[0], pieces[1])
        step(x2, ends, 2, result(ends, (0, 1)))
        for p in (2, 3):
            step(x2, (pieces[p],), 2, result((pieces[p],), (p,)))
        flush()
        pltpu.make_async_copy(outb.at[t], maps.at[t], out_s.at[t]).start()

    for t in range(ticks):
        @pl.when(has_up)
        def _():
            up_copy(t).wait_send()

        @pl.when(has_down)
        def _():
            down_copy(t).wait_send()

        for p in range(count):
            @pl.when(has_next)
            def _():
                shift_copy(held if t == 0 else outb.at[t - 1], t, p).wait_send()

            if t < last:
                @pl.when(relays)
                def _():
                    relay_copy(t, p).wait_send()

                @pl.when(direct)
                def _():
                    stash_copy(t, p).wait_send()

                @pl.when(decoder)
                def _():
                    keep_copy(t, p).wait()
            else:
                @pl.when(encoder)
                def _():
                    stash_copy(t, p).wait_send()

                @pl.when(decoder)
                def _():
                    stash_copy(t, p).wait_recv()
        pltpu.make_async_copy(outb.at[t], maps.at[t], out_s.at[t]).wait()


def on_device(held_maps, held_skips, arrivals, kernels, biases):
    ticks, _, rows, w, c = held_skips.shape
    flat = rows * w
    any_spec = pl.BlockSpec(memory_space=pl.ANY)
    shape = jax.ShapeDtypeStruct((ticks, flat, c), BF16)
    dma = pltpu.SemaphoreType.DMA
    maps, stash = pl.pallas_call(
        functools.partial(body, ticks, rows, w, c),
        out_shape=(shape, shape),
        in_specs=[any_spec] * 5,
        out_specs=(any_spec, any_spec),
        scratch_shapes=[
            pltpu.VMEM((ticks, flat, c), BF16),
            pltpu.VMEM((ticks, flat, c), BF16),
            pltpu.VMEM((ticks, 2, 3 * w, c), BF16),
            pltpu.VMEM((ticks, 2, 3 * w, c), BF16),
            pltpu.VMEM((3, 9 * c, c), BF16),
            pltpu.VMEM((3, 1, c), F32),
            pltpu.VMEM(((rows + 6) * w, 3 * c), BF16),
            pltpu.VMEM(((rows + 4) * w, 3 * c), BF16),
            pltpu.VMEM(((rows + 2) * w, 3 * c), BF16),
            pltpu.VMEM((ticks, flat, c), BF16),
            dma((ticks, 4)),
            dma((ticks, 4)),
            dma((ticks, 2)),
            dma((ticks, 2)),
            dma((ticks, 4)),
            dma((ticks, 4)),
            dma((ticks, 4)),
            dma((ticks,)),
            dma((3,)),
            dma((1,)),
            dma((1,)),
        ],
        compiler_params=pltpu.CompilerParams(
            collective_id=0, has_side_effects=True, vmem_limit_bytes=63 * 1024 * 1024
        ),
    )(
        held_maps.reshape(flat, c),
        held_skips.reshape(ticks, flat, c),
        arrivals.reshape(ticks, flat, c),
        kernels.reshape(3, 9 * c, c),
        biases.reshape(3, 1, c),
    )
    decoder = lax.axis_index("segment") >= lax.axis_size("segment") // 2
    stash = jnp.where(decoder, stash, jnp.zeros_like(stash))
    full = (ticks, 1, rows, w, c)
    return maps.reshape(full), stash.reshape(full)


def solution(mesh):
    placed = (
        P("segment", "rows", None, None),
        P(None, "segment", "rows", None, None),
        P(None, "rows", None, None),
        P("segment", None, None, None, None),
        P("segment", None, None),
    )
    return jax.shard_map(
        on_device,
        mesh=mesh,
        in_specs=placed,
        out_specs=(P(None, "segment", "rows", None, None), P(None, "segment", "rows", None, None)),
        check_vma=False,
    )
```

```python
import functools

import jax
import jax.numpy as jnp
from jax import lax
from jax.experimental import pallas as pl
from jax.experimental.pallas import tpu as pltpu
from jax.sharding import PartitionSpec as P

BF16 = jnp.bfloat16
F32 = jnp.float32


def body(
    ticks, rows, w, c,
    held, skips_in, arrivals, kern, bias_in,
    maps, stash,
    inc, sk, sec, halo, kv, bias, x0, x1, x2, outb,
    inc_rs, shift_ss, halo_ss, halo_rs, st_ss, st_rs, fwd_ss, out_s, k_s, sk_s, b_s,
):
    n = lax.axis_size("segment")
    nz = lax.axis_size("rows")
    s = lax.axis_index("segment")
    z = lax.axis_index("rows")
    half = n // 2
    last = ticks - 1
    encoder = s < half
    decoder = s >= half
    middle = s == half
    has_next = s < n - 1
    has_prev = s >= 1
    has_up = z >= 1
    has_down = z < nz - 1
    relayed = encoder & (s % 2 == 1) & (s < half - 1)
    relays = encoder & (s % 2 == 0) & (s >= 2)
    from_relay = (s > half) & (s % 2 == 0)
    direct = encoder & (s % 2 == 0) & (s < half - 1)
    mirror = n - 1 - s
    q = 3
    h = (rows - 2 * q + 1) // 2
    pieces = ((0, q), (rows - q, q), (q, h), (q + h, rows - 2 * q - h))
    count = len(pieces)

    def at(segment, row):
        return {"segment": segment, "rows": row}

    barrier = pltpu.get_barrier_semaphore()
    links = (
        (has_next, s + 1, z),
        (has_prev, s - 1, z),
        (encoder | decoder, mirror, z),
        (relays | from_relay, n - s, z),
        (has_up, s, z - 1),
        (has_down, s, z + 1),
    )
    partners = 0
    for cond, seg, row in links:
        @pl.when(cond)
        def _():
            pl.semaphore_signal(barrier, inc=1, device_id=at(seg, row), device_id_type=pl.DeviceIdType.MESH)
        partners = partners + cond.astype(jnp.int32)

    k_copies = [pltpu.make_async_copy(kern.at[l], kv.at[l], k_s.at[l]) for l in range(3)]
    for copy in k_copies:
        copy.start()
    bias_copy = pltpu.make_async_copy(bias_in, bias, b_s.at[0])
    bias_copy.start()
    skip_copy = pltpu.make_async_copy(skips_in, sk, sk_s.at[0])

    @pl.when(decoder)
    def _():
        skip_copy.start()

    @pl.when(s == 0)
    def _():
        for t in range(ticks):
            for p, (r, m) in enumerate(pieces):
                pltpu.make_async_copy(
                    arrivals.at[t, pl.ds(r * w, m * w)], inc.at[t, pl.ds(r * w, m * w)], inc_rs.at[t, p]
                ).start()

    pl.semaphore_wait(barrier, partners)

    def remote(src, dst, ss, rs, seg, row):
        return pltpu.make_async_remote_copy(
            src_ref=src, dst_ref=dst, send_sem=ss, recv_sem=rs, device_id=at(seg, row),
            device_id_type=pl.DeviceIdType.MESH,
        )

    def shift_copy(src, t, p):
        r, m = pieces[p]
        rng = pl.ds(r * w, m * w)
        return remote(src.at[rng], inc.at[t, rng], shift_ss.at[t, p], inc_rs.at[t, p], s + 1, z)

    def stash_copy(t, p):
        r, m = pieces[p]
        rng = pl.ds(r * w, m * w)
        return remote(outb.at[t, rng], stash.at[t, rng], st_ss.at[t, p], st_rs.at[t, p], mirror, z)

    def relay_copy(t, p):
        r, m = pieces[p]
        rng = pl.ds(r * w, m * w)
        return remote(inc.at[t + 1, rng], stash.at[t, rng], fwd_ss.at[t, p], st_rs.at[t, p], n - s, z)

    def keep_copy(t, p):
        r, m = pieces[p]
        rng = pl.ds(r * w, m * w)
        return pltpu.make_async_copy(inc.at[t + 1, rng], stash.at[t, rng], st_rs.at[t, p])

    @pl.when(has_next)
    def _():
        for p in range(count):
            shift_copy(held, 0, p).start()

    e = 3 * w

    def up_copy(t):
        return remote(sec.at[t, 0], halo.at[t, 1], halo_ss.at[t, 0], halo_rs.at[t, 1], s, z - 1)

    def down_copy(t):
        return remote(sec.at[t, 1], halo.at[t, 0], halo_ss.at[t, 1], halo_rs.at[t, 0], s, z + 1)

    @pl.when(encoder)
    def _():
        sk[...] = jnp.zeros_like(sk)

    @pl.when(jnp.logical_not(has_up))
    def _():
        for t in range(ticks):
            halo[t, 0] = jnp.zeros((e, c), BF16)

    @pl.when(jnp.logical_not(has_down))
    def _():
        for t in range(ticks):
            halo[t, 1] = jnp.zeros((e, c), BF16)

    def put(dst, row, a):
        m = a.shape[0]
        rng = pl.ds(row * w, m)
        dst[rng, c : 2 * c] = a.astype(BF16)
        sub = lax.broadcasted_iota(jnp.int32, (m // w, 8, c), 1)
        left = pltpu.roll(a, 1, 0).reshape(m // w, w, c)
        first = jnp.where(sub == 0, 0.0, left[:, 0:8])
        dst[rng, 0:c] = jnp.concatenate([first, left[:, 8:]], axis=1).reshape(m, c).astype(BF16)
        right = pltpu.roll(a, m - 1, 0).reshape(m // w, w, c)
        final = jnp.where(sub == 7, 0.0, right[:, w - 8 :])
        dst[rng, 2 * c : 3 * c] = jnp.concatenate([right[:, 0 : w - 8], final], axis=1).reshape(m, c).astype(BF16)

    def silu(v):
        return v * (0.5 + 0.5 * jnp.tanh(0.5 * v))

    up_i = has_up.astype(jnp.int32)
    down_i = has_down.astype(jnp.int32)
    pending = []

    def flush():
        while pending:
            pending.pop(0)()

    def step(src, base, spans, l, finish):
        for b, m in spans:
            for o in range(0, m, 3):
                k = min(3, m - o)
                acc = sum(jnp.dot(src[pl.ds((base + b + o + d) * w, k * w), :], kv[l, pl.ds(3 * c * d, 3 * c), :], preferred_element_type=F32) for d in range(3))
                flush()
                pending.append(functools.partial(finish, b + o, k, acc))

    def store(dst, shift, l):
        def finish(b, m, acc):
            v = silu(acc + bias[l])
            low, high = max(0, -b), max(0, b + m - rows)
            if low or high:
                idx = lax.broadcasted_iota(jnp.int32, v.shape, 0)
                inside = jnp.where(idx < low * w, up_i, jnp.where(idx >= (m - high) * w, down_i, 1))
                v = jnp.where(inside > 0, v, 0.0)
            put(dst, b + shift, v)

        return finish

    for t in range(ticks):
        mid_t = middle if t >= 1 else None

        def joined(p):
            r, m = pieces[p]
            rng = pl.ds(r * w, m * w)
            x = inc[t, rng].astype(F32)
            add = sk[t, rng].astype(F32)
            if mid_t is not None:
                add = jnp.where(mid_t, x, add)
            return (x + add).astype(BF16)

        def arrived(p):
            r, m = pieces[p]
            view = inc.at[t, pl.ds(r * w, m * w)]
            pltpu.make_async_copy(view, view, inc_rs.at[t, p]).wait()
            if t >= 1:
                @pl.when(relays)
                def _():
                    relay_copy(t - 1, p).start()

                @pl.when(middle)
                def _():
                    keep_copy(t - 1, p).start()

        def emit(p):
            if t < last:
                @pl.when(has_next)
                def _():
                    shift_copy(outb.at[t], t + 1, p).start()

                @pl.when(direct)
                def _():
                    stash_copy(t, p).start()
            else:
                @pl.when(encoder)
                def _():
                    stash_copy(t, p).start()

        def finish_out(b, m, acc):
            own = x0[pl.ds((3 + b) * w, m * w), c : 2 * c].astype(F32)
            outb[t, pl.ds(b * w, m * w)] = (own + (acc + bias[2])).astype(BF16)

        if t == 0:
            @pl.when(decoder)
            def _():
                skip_copy.wait()

        arrived(0)
        top = joined(0)
        sec[t, 0] = top

        @pl.when(has_up)
        def _():
            up_copy(t).start()

        arrived(1)
        bottom = joined(1)
        sec[t, 1] = bottom

        @pl.when(has_down)
        def _():
            down_copy(t).start()

        put(x0, 3, top.astype(F32))
        put(x0, 3 + rows - q, bottom.astype(F32))
        arrived(2)
        put(x0, 3 + pieces[2][0], joined(2).astype(F32))
        if t == 0:
            bias_copy.wait()
            k_copies[0].wait()
        a_end = q + h - 2
        step(x0, 2, ((1, a_end),), 0, store(x1, 2, 0))
        arrived(3)
        put(x0, 3 + pieces[3][0], joined(3).astype(F32))
        step(x0, 2, ((1 + a_end, rows - 2 - a_end),), 0, store(x1, 2, 0))

        @pl.when(has_down)
        def _():
            remote(sec.at[t, 0], halo.at[t, 1], halo_ss.at[t, 0], halo_rs.at[t, 1], s, z).wait_recv()

        @pl.when(has_up)
        def _():
            remote(sec.at[t, 1], halo.at[t, 0], halo_ss.at[t, 1], halo_rs.at[t, 0], s, z).wait_recv()

        put(x0, 0, halo[t, 0].astype(F32))
        put(x0, 3 + rows, halo[t, 1].astype(F32))
        step(x0, 2, ((-2, 3), (rows - 1, 3)), 0, store(x1, 2, 0))
        if t == 0:
            k_copies[1].wait()
        step(x1, 1, ((5, rows - 10),), 1, store(x2, 1, 1))
        step(x1, 1, ((-1, 6), (rows - 5, 6)), 1, store(x2, 1, 1))
        if t == 0:
            k_copies[2].wait()
        step(x2, 0, (pieces[0], pieces[1]), 2, finish_out)
        flush()
        emit(0)
        emit(1)
        for p in (2, 3):
            step(x2, 0, (pieces[p],), 2, finish_out)
            flush()
            emit(p)
        flush()
        pltpu.make_async_copy(outb.at[t], maps.at[t], out_s.at[t]).start()

    for t in range(ticks):
        @pl.when(has_up)
        def _():
            up_copy(t).wait_send()

        @pl.when(has_down)
        def _():
            down_copy(t).wait_send()

        for p in range(count):
            @pl.when(has_next)
            def _():
                shift_copy(held if t == 0 else outb.at[t - 1], t, p).wait_send()

            if t < last:
                @pl.when(relays)
                def _():
                    relay_copy(t, p).wait_send()

                @pl.when(direct)
                def _():
                    stash_copy(t, p).wait_send()

                @pl.when(decoder)
                def _():
                    keep_copy(t, p).wait()
            else:
                @pl.when(encoder)
                def _():
                    stash_copy(t, p).wait_send()

                @pl.when(decoder)
                def _():
                    stash_copy(t, p).wait_recv()
        pltpu.make_async_copy(outb.at[t], maps.at[t], out_s.at[t]).wait()


def on_device(held_maps, held_skips, arrivals, kernels, biases):
    ticks, _, rows, w, c = held_skips.shape
    flat = rows * w
    any_spec = pl.BlockSpec(memory_space=pl.ANY)
    shape = jax.ShapeDtypeStruct((ticks, flat, c), BF16)
    dma = pltpu.SemaphoreType.DMA
    maps, stash = pl.pallas_call(
        functools.partial(body, ticks, rows, w, c),
        out_shape=(shape, shape),
        in_specs=[any_spec] * 5,
        out_specs=(any_spec, any_spec),
        scratch_shapes=[
            pltpu.VMEM((ticks, flat, c), BF16),
            pltpu.VMEM((ticks, flat, c), BF16),
            pltpu.VMEM((ticks, 2, 3 * w, c), BF16),
            pltpu.VMEM((ticks, 2, 3 * w, c), BF16),
            pltpu.VMEM((3, 9 * c, c), BF16),
            pltpu.VMEM((3, 1, c), F32),
            pltpu.VMEM(((rows + 6) * w, 3 * c), BF16),
            pltpu.VMEM(((rows + 4) * w, 3 * c), BF16),
            pltpu.VMEM(((rows + 2) * w, 3 * c), BF16),
            pltpu.VMEM((ticks, flat, c), BF16),
            dma((ticks, 4)),
            dma((ticks, 4)),
            dma((ticks, 2)),
            dma((ticks, 2)),
            dma((ticks, 4)),
            dma((ticks, 4)),
            dma((ticks, 4)),
            dma((ticks,)),
            dma((3,)),
            dma((1,)),
            dma((1,)),
        ],
        compiler_params=pltpu.CompilerParams(
            collective_id=0, has_side_effects=True, vmem_limit_bytes=63 * 1024 * 1024
        ),
    )(
        held_maps.reshape(flat, c),
        held_skips.reshape(ticks, flat, c),
        arrivals.reshape(ticks, flat, c),
        kernels.reshape(3, 9 * c, c),
        biases.reshape(3, 1, c),
    )
    decoder = lax.axis_index("segment") >= lax.axis_size("segment") // 2
    stash = jnp.where(decoder, stash, jnp.zeros_like(stash))
    full = (ticks, 1, rows, w, c)
    return maps.reshape(full), stash.reshape(full)


def solution(mesh):
    placed = (
        P("segment", "rows", None, None),
        P(None, "segment", "rows", None, None),
        P(None, "rows", None, None),
        P("segment", None, None, None, None),
        P("segment", None, None),
    )
    return jax.shard_map(
        on_device,
        mesh=mesh,
        in_specs=placed,
        out_specs=(P(None, "segment", "rows", None, None), P(None, "segment", "rows", None, None)),
        check_vma=False,
    )
```
